32 devices in a mesh: row: 8 (over z, y), col: 4 (over x, core).
Axes of the slice: x: 2, y: 2, z: 4, core: 2. Of those that a mesh axis runs over, the one named last changes fastest.
Arguments:
- front: float32 [8, 8, 128, 16, 4, 128], P(None, 'row', None, None, 'col'), as said below
- updates: float32 [2, 8, 8, 128, 12, 4, 128], P(None, None, 'row', None, None, 'col'), as said below
- maps: int32 [2, 48], replicated, may hold values from 0 to 63, as said below
Outputs:
- factor: float32 [8, 8, 128, 16, 4, 128], P(None, 'row', None, None, 'col')
The draws below stay inside these ranges and needn't reach their ends.
Inputs may be any that keep to these rules, and one draw needn't show every extreme that they name: maps[k, j] is strictly increasing in j, and maps[k, j] - j is the same within each aligned group of 4 blocks. For each child and each c, of the blocks j with j % 4 == c at most 6 have maps[k, j] % 4 equal to any one value, and exactly 6 do for some value. updates[k] is child k's symmetric update matrix with its row block i placed at parent row block maps[k, i]; parent row blocks that no block of child k maps to are zero. front is symmetric, and with the updates added every block that is factored is positive definite.
All inputs are finite; a program needn't handle non-finite values.
Results may differ from the reference program's by a relative error of at most 0.0003.
Values sent between devices are 32-bit elements; how exact they have to be, the bound alone decides.
A program may use at most 192 MiB of HBM per device.

```python
import jax
import jax.numpy as jnp
from jax import lax

BLK = 128
NF = 8192
NC = 6144
NP = 2
NBP = 64
NBC = 48
PR = 8
PC = 16
CC = 12
W = 512
N_ROW = 8
N_COL = 4


def symmetric(key, length):
    base_draw = jax.random.normal(key, (length, length), jnp.float32)
    return (base_draw + base_draw.T) * 0.70710678


def gram_part(key):
    columns = NP * W // 4
    factors = jax.random.randint(key, (NF, columns), -3, 4).astype(jnp.float32)
    spread = 4.0
    gram = jnp.dot(factors, factors.T, precision=lax.Precision.HIGHEST, preferred_element_type=jnp.float32)
    return gram * (16.0 * NF ** 0.5 / (spread * columns))


def child_map(key):
    groups = NBC // N_COL
    capacity = groups // 2
    subkeys = jax.random.split(key, 4)
    first_count = jax.random.randint(subkeys[0], (), 0, groups - capacity + 1)
    second = jax.random.randint(subkeys[1], (), 0, groups - capacity - first_count + 1)
    counts = jnp.stack([jnp.int32(capacity), first_count, second, groups - capacity - first_count - second])
    bounds = jnp.cumsum(counts)
    positions = jnp.arange(groups, dtype=jnp.int32)
    run_index = jnp.sum((positions[:, None] >= bounds[None, :3]).astype(jnp.int32), axis=1)
    residue_order = jax.random.permutation(subkeys[2], N_COL).astype(jnp.int32)
    residue = jnp.sum(jnp.where(run_index[:, None] == jnp.arange(N_COL, dtype=jnp.int32)[None, :], residue_order[None, :], 0), axis=1)
    previous = jnp.concatenate([jnp.zeros((1,), jnp.int32), residue[:-1]])
    increment = (residue - previous) % N_COL
    spare_groups = min(groups - 1, (NBP - NBC - N_COL * (N_COL - 1)) // N_COL)
    extras = jax.random.randint(subkeys[3], (groups,), 0, 2)
    extras = jnp.where((positions >= 1) & (positions <= spare_groups), extras, 0)
    offsets = jnp.cumsum(increment + N_COL * extras)
    blocks = jnp.arange(NBC, dtype=jnp.int32)
    return (blocks + jnp.repeat(offsets, N_COL)).astype(jnp.int32)


def make_maps(key):
    base_key = jax.random.fold_in(key, 7)
    return jnp.stack([child_map(jax.random.fold_in(base_key, 0)), child_map(jax.random.fold_in(base_key, 1))])


def draw_maps(key, part):
    return make_maps(key)


def draw_front(key, part):
    matrix = symmetric(jax.random.fold_in(key, 3), NF)
    diagonal = jax.random.uniform(jax.random.fold_in(key, 4), (NF,), jnp.float32, 4.0, 8.0) * NF ** 0.5
    diagonal_index = jnp.arange(NF)
    matrix = matrix.at[diagonal_index, diagonal_index].set(diagonal)
    matrix = matrix + gram_part(jax.random.fold_in(key, 5))
    return matrix.reshape(PR, N_ROW, BLK, PC, N_COL, BLK)


def draw_updates(key, part):
    parents = make_maps(key)
    stacked = []
    for member in range(2):
        values = symmetric(jax.random.fold_in(key, 20 + member), NC) * 0.7
        matches = parents[member][None, :] == jnp.arange(NBP, dtype=jnp.int32)[:, None]
        source = jnp.sum(jnp.where(matches, jnp.arange(NBC, dtype=jnp.int32)[None, :], 0), axis=1)
        present = jnp.any(matches, axis=1).astype(jnp.float32)
        placed = values.reshape(NBC, BLK, NC)[source] * present[:, None, None]
        stacked.append(placed.reshape(PR, N_ROW, BLK, CC, N_COL, BLK))
    return jnp.stack(stacked)


def setup_inputs(seed: int = 0) -> dict:
    splits = jax.random.split(jax.random.key(seed), 4)
    front = draw_front(jax.random.fold_in(splits[3], 71), 0)
    updates = draw_updates(jax.random.fold_in(splits[3], 71), 0)
    maps = draw_maps(jax.random.fold_in(splits[3], 71), 0)
    return dict(front=front, updates=updates, maps=maps)


highest = lax.Precision.HIGHEST

def extend(matrix, update, parent_of):
    row_total = matrix.shape[0]
    blocks = matrix.reshape(row_total, NBP, BLK)
    blocks = blocks.at[:, parent_of].add(update.reshape(row_total, NBC, BLK))
    return blocks.reshape(row_total, NF)

def reference(front, updates, maps):
    matrix = front.reshape(NF, NF)
    children = updates.reshape(2, NF, NC)
    for member in range(2):
        matrix = extend(matrix, children[member], maps[member])
    position = jnp.arange(NF, dtype=jnp.int32)
    for panel_index in range(NP):
        begin_at = panel_index * W
        finish = begin_at + W
        square = matrix[begin_at:finish, begin_at:finish]
        lower_factor = jnp.linalg.cholesky(square)
        inverse = lax.linalg.triangular_solve(lower_factor, jnp.eye(W, dtype=jnp.float32), left_side=True, lower=True)
        left_factor = jnp.dot(matrix[:, begin_at:finish].astype(jnp.float32), inverse.T.astype(jnp.float32), precision=highest, preferred_element_type=jnp.float32)
        right_factor = jnp.dot(inverse.astype(jnp.float32), matrix[begin_at:finish, :].astype(jnp.float32), precision=highest, preferred_element_type=jnp.float32)
        beyond = position >= finish
        trailing = jnp.dot(jnp.where(beyond[:, None], left_factor, 0.0).astype(jnp.float32), jnp.where(beyond[None, :], right_factor, 0.0).astype(jnp.float32), precision=highest, preferred_element_type=jnp.float32)
        matrix = matrix - trailing
        inside = (position >= begin_at) & (position < finish)
        diag_rows = lower_factor[jnp.clip(position - begin_at, 0, W - 1)]
        column_vals = jnp.where(beyond[:, None], left_factor, jnp.where(inside[:, None], diag_rows, 0.0))
        matrix = matrix.at[:, begin_at:finish].set(column_vals)
        matrix = jnp.where(inside[:, None] & beyond[None, :], 0.0, matrix)
    return matrix.reshape(front.shape)
```

```python
import functools

import jax
import jax.numpy as jnp
from jax import lax
from jax.experimental import pallas as pl
from jax.experimental.pallas import tpu as pltpu
from jax.sharding import PartitionSpec as P

NP = 2
highest = lax.Precision.HIGHEST
VMEM_LIMIT = 56 * 1024 * 1024


def split(value):
    high = value.astype(jnp.bfloat16)
    low = (value - high.astype(jnp.float32)).astype(jnp.bfloat16)
    return high, low


def dims(transposed):
    return (((1,), (1 if transposed else 0,)), ((), ()))


def product3(left_pair, right_pair, transposed=False):
    def one(a, b):
        return lax.dot_general(a, b, dims(transposed), preferred_element_type=jnp.float32)

    return (
        one(left_pair[0], right_pair[0])
        + one(left_pair[0], right_pair[1])
        + one(left_pair[1], right_pair[0])
    )


def product(a, b, transposed=False):
    return lax.dot_general(
        a, b, dims(transposed), precision=highest, preferred_element_type=jnp.float32
    )


def pack_kernel(child_cols, cap, blk, table, updates_ref, one_ref, two_ref, three_ref):
    for turn, out_ref in enumerate((one_ref, two_ref, three_ref)):
        for member in range(2):
            for slot in range(cap):
                source = table[(turn + 1) * 2 * cap + member * cap + slot]
                out_ref[member * cap + slot] = updates_ref[
                    member, 0, pl.ds(source, blk, stride=child_cols), :
                ]


def pack(table, updates, cap):
    part_rows, blk, child_cols = updates.shape[1], updates.shape[3], updates.shape[4]
    flat = updates.reshape(2, part_rows, blk * child_cols, blk)
    return pl.pallas_call(
        functools.partial(pack_kernel, child_cols, cap, blk),
        grid_spec=pltpu.PrefetchScalarGridSpec(
            num_scalar_prefetch=1,
            grid=(part_rows,),
            in_specs=[pl.BlockSpec((2, 1, blk * child_cols, blk), lambda a, t: (0, a, 0, 0))],
            out_specs=[pl.BlockSpec((2 * cap, blk, blk), lambda a, t: (0, a, 0))] * 3,
        ),
        out_shape=[jax.ShapeDtypeStruct((2 * cap, part_rows * blk, blk), jnp.float32)] * 3,
        compiler_params=pltpu.CompilerParams(vmem_limit_bytes=VMEM_LIMIT),
        name="pack",
    )(table, flat)


def assemble_kernel(part_cols, child_cols, blk, table, front_ref, updates_ref, *refs):
    received, out_ref = refs[:3], refs[3]
    for slot in range(part_cols):
        cols = slice(slot * blk, (slot + 1) * blk)
        out_ref[:, cols] = front_ref[0, pl.ds(slot, blk, stride=part_cols), :]
        for member in range(2):
            turn = table[(member * part_cols + slot) * 2]
            index = table[(member * part_cols + slot) * 2 + 1]

            @pl.when(turn == 0)
            def _():
                out_ref[:, cols] += updates_ref[member, 0, pl.ds(index, blk, stride=child_cols), :]

            for step in range(3):

                @pl.when(turn == step + 1)
                def _():
                    out_ref[:, cols] += received[step][index]


def assemble(table, front, updates, received):
    part_rows, blk, part_cols = front.shape[0], front.shape[2], front.shape[3]
    child_cols = updates.shape[4]
    slots = received[0].shape[0]
    return pl.pallas_call(
        functools.partial(assemble_kernel, part_cols, child_cols, blk),
        grid_spec=pltpu.PrefetchScalarGridSpec(
            num_scalar_prefetch=1,
            grid=(part_rows,),
            in_specs=[
                pl.BlockSpec((1, blk * part_cols, blk), lambda a, t: (a, 0, 0)),
                pl.BlockSpec((2, 1, blk * child_cols, blk), lambda a, t: (0, a, 0, 0)),
            ]
            + [pl.BlockSpec((slots, blk, blk), lambda a, t: (0, a, 0))] * 3,
            out_specs=pl.BlockSpec((blk, part_cols * blk), lambda a, t: (a, 0)),
        ),
        out_shape=jax.ShapeDtypeStruct((part_rows * blk, part_cols * blk), jnp.float32),
        compiler_params=pltpu.CompilerParams(vmem_limit_bytes=VMEM_LIMIT),
        name="assemble",
    )(
        table,
        front.reshape(part_rows, blk * part_cols, blk),
        updates.reshape(2, part_rows, blk * child_cols, blk),
        *received,
    )


def eliminate(block):
    size = block.shape[0]
    row_ids = lax.broadcasted_iota(jnp.int32, (size, size), 0)
    col_ids = lax.broadcasted_iota(jnp.int32, (size, size), 1)
    tiles = size // 8
    upper = [block[8 * t : 8 * t + 8, :] for t in range(tiles)]
    start = (row_ids == col_ids).astype(jnp.float32)
    solved = [start[8 * t : 8 * t + 8, :] for t in range(tiles)]
    local = lax.broadcasted_iota(jnp.int32, (8, size), 0)
    for j in range(size):
        home, inner = j // 8, j % 8
        pivot_row = upper[home][inner : inner + 1, :]
        solved_row = solved[home][inner : inner + 1, :]
        scale = 1.0 / pivot_row[:, j : j + 1]
        for t in range(home, tiles):
            if t == home and inner == 7:
                continue
            factor = upper[t][:, j : j + 1] * scale
            if t == home:
                factor = jnp.where(local[:, :1] > inner, factor, 0.0)
            upper[t] = upper[t] - factor * pivot_row
            solved[t] = solved[t] - factor * solved_row
    upper = jnp.concatenate(upper, axis=0)
    solved = jnp.concatenate(solved, axis=0)
    diagonal = jnp.sum(jnp.where(row_ids == col_ids, upper, 0.0), axis=1, keepdims=True)
    scale = 1.0 / jnp.sqrt(diagonal)
    lower = jnp.where(col_ids >= row_ids, upper * scale, 0.0).T
    return lower, solved * scale


def factor_kernel(blk, square_ref, lower_ref, inverse_ref, work):
    size = square_ref.shape[0]
    count = size // blk
    work[...] = square_ref[...]
    lower_ref[...] = jnp.zeros_like(lower_ref)
    inverse_ref[...] = jnp.zeros_like(inverse_ref)
    rows = lax.broadcasted_iota(jnp.int32, (size, blk), 0)

    def step(k, carry):
        begin = pl.multiple_of(k * blk, blk)
        here = pl.ds(begin, blk)
        diag_lower, diag_inverse = eliminate(work[here, here])
        inverse_ref[here, here] = diag_inverse
        column = product(work[:, here], diag_inverse, True)
        column = jnp.where(rows >= begin + blk, column, 0.0)
        lower_ref[:, here] = column
        lower_ref[here, here] = diag_lower
        for q in range(0, size, 256):
            piece = slice(q, q + 256)

            @pl.when(q + 256 > begin + blk)
            def _():
                work[piece, :] -= product(lower_ref[piece, here] * (rows[piece] >= begin + blk), column, True)

        return carry

    lax.fori_loop(0, count, step, 0)

    def substitute(i, carry):
        begin = pl.multiple_of(i * blk, blk)
        here = pl.ds(begin, blk)
        cols = lax.broadcasted_iota(jnp.int32, (blk, size), 1)
        diag_inverse = inverse_ref[here, here]
        strip = jnp.where(cols < begin, lower_ref[here, :], 0.0)
        total = product(strip, inverse_ref[...])
        update = product(diag_inverse, total)
        inverse_ref[here, :] -= update
        return carry

    lax.fori_loop(1, count, substitute, 0)


def factorize(square, blk):
    size = square.shape[0]
    shape = jax.ShapeDtypeStruct((size, size), jnp.float32)
    return pl.pallas_call(
        functools.partial(factor_kernel, blk),
        out_shape=[shape, shape],
        scratch_shapes=[pltpu.VMEM((size, size), jnp.float32)],
        compiler_params=pltpu.CompilerParams(vmem_limit_bytes=VMEM_LIMIT),
        name="factorize",
    )(square)


def right_kernel(inverse_ref, top_ref, high_ref, low_ref, inv_high, inv_low):
    @pl.when(pl.program_id(0) == 0)
    def _():
        inv_high[...], inv_low[...] = split(inverse_ref[...])

    result = product3((inv_high[...], inv_low[...]), split(top_ref[...]))
    high_ref[...], low_ref[...] = split(result)


def right_side(inverse, top, skip, tile):
    size, cols = top.shape
    out = jax.ShapeDtypeStruct((size, cols - skip), jnp.bfloat16)
    return pl.pallas_call(
        right_kernel,
        grid=((cols - skip) // tile,),
        in_specs=[
            pl.BlockSpec((size, size), lambda n: (0, 0)),
            pl.BlockSpec((size, tile), lambda n: (0, n + skip // tile)),
        ],
        out_specs=[pl.BlockSpec((size, tile), lambda n: (0, n))] * 2,
        out_shape=[out, out],
        scratch_shapes=[pltpu.VMEM((size, size), jnp.bfloat16)] * 2,
        compiler_params=pltpu.CompilerParams(vmem_limit_bytes=VMEM_LIMIT),
        name="right",
    )(inverse, top)


def final_kernel(
    part_cols, blk, row_count, col_count, place,
    panel_ref, matrix_ref, inverse_ref, lower_ref, high_ref, low_ref,
    out_ref, inv_high, inv_low, left_ref,
):
    step = pl.program_id(0)
    row_blocks = out_ref.shape[0]
    panel_blocks = NP * col_count

    @pl.when(step == 0)
    def _():
        inv_high[...], inv_low[...] = split(inverse_ref[...])

    left_ref[...] = product3(split(panel_ref[...]), (inv_high[...], inv_low[...]), True)
    left_pair = split(left_ref[...])
    for pair in range(NP, part_cols, 2):
        cols = slice((pair - NP) * blk, (pair - NP + 2) * blk)
        trailing = product3(left_pair, (high_ref[:, cols], low_ref[:, cols]))
        updated = matrix_ref[:, pair * blk : (pair + 2) * blk] - trailing
        for t in range(row_blocks):
            for half in range(2):
                out_ref[t, pl.ds(pair + half, blk, stride=part_cols), :] = updated[
                    t * blk : (t + 1) * blk, half * blk : (half + 1) * blk
                ]
    for t in range(row_blocks):
        block_row = (step * row_blocks + t) * row_count + place[0]
        for slot in range(NP):
            start = pl.multiple_of((slot * col_count + place[1]) * blk, blk)
            out_ref[t, pl.ds(slot, blk, stride=part_cols), :] = left_ref[
                t * blk : (t + 1) * blk, pl.ds(start, blk)
            ]

        @pl.when(block_row < panel_blocks)
        def _():
            out_ref[t] = jnp.zeros_like(out_ref[t])
            begin = pl.multiple_of(block_row * blk, blk)
            for slot in range(NP):
                start = pl.multiple_of((slot * col_count + place[1]) * blk, blk)
                out_ref[t, pl.ds(slot, blk, stride=part_cols), :] = lower_ref[
                    pl.ds(begin, blk), pl.ds(start, blk)
                ]


def finish(place, panel, matrix, inverse, lower, high, low, row_count, col_count, blk):
    rows, cols = matrix.shape
    part_rows, part_cols = rows // blk, cols // blk
    size = inverse.shape[0]
    group = 2 if part_rows % 2 == 0 else 1

    def resident(shape):
        return pl.BlockSpec(shape, lambda a, t: (0, 0), pipeline_mode=pl.Buffered(1))

    def kernel(place, *refs):
        final_kernel(part_cols, blk, row_count, col_count, place, *refs)

    return pl.pallas_call(
        kernel,
        grid_spec=pltpu.PrefetchScalarGridSpec(
            num_scalar_prefetch=1,
            grid=(part_rows // group,),
            in_specs=[
                pl.BlockSpec((group * blk, size), lambda a, t: (a, 0)),
                pl.BlockSpec((group * blk, cols), lambda a, t: (a, 0)),
                resident((size, size)),
                resident((size, size)),
                resident(high.shape),
                resident(low.shape),
            ],
            out_specs=pl.BlockSpec((group, blk * part_cols, blk), lambda a, t: (a, 0, 0)),
            scratch_shapes=[
                pltpu.VMEM((size, size), jnp.bfloat16),
                pltpu.VMEM((size, size), jnp.bfloat16),
                pltpu.VMEM((group * blk, size), jnp.float32),
            ],
        ),
        out_shape=jax.ShapeDtypeStruct((part_rows, blk * part_cols, blk), jnp.float32),
        compiler_params=pltpu.CompilerParams(vmem_limit_bytes=VMEM_LIMIT),
        name="finish",
    )(place, panel, matrix, inverse, lower, high, low)


def tables(maps, col_index, col_count, child_cols, part_cols, cap):
    offsets = maps[:, ::col_count] - col_count * jnp.arange(child_cols, dtype=jnp.int32)[None, :]
    turn = offsets % col_count
    groups = jnp.arange(child_cols, dtype=jnp.int32)
    same = (turn[:, :, None] == turn[:, None, :]) & (groups[None, None, :] < groups[None, :, None])
    rank = jnp.sum(same.astype(jnp.int32), axis=2)
    turns = jnp.arange(col_count, dtype=jnp.int32)
    slots = jnp.arange(cap, dtype=jnp.int32)
    hot = (turn[None, :, None, :] == turns[:, None, None, None]) & (
        rank[None, :, None, :] == slots[None, None, :, None]
    )
    send = jnp.sum(jnp.where(hot, groups[None, None, None, :], 0), axis=3).reshape(-1)
    parents = jnp.arange(part_cols, dtype=jnp.int32) * col_count + col_index
    match = maps[:, None, :] == parents[None, :, None]
    spread = jnp.repeat(groups, col_count)
    group = jnp.sum(jnp.where(match, spread[None, None, :], 0), axis=2)
    present = jnp.any(match, axis=2)
    pick = group[:, :, None] == groups[None, None, :]
    kind = jnp.sum(jnp.where(pick, turn[:, None, :], 0), axis=2)
    order = jnp.sum(jnp.where(pick, rank[:, None, :], 0), axis=2)
    order = jnp.where(kind == 0, group, order + cap * jnp.arange(2, dtype=jnp.int32)[:, None])
    kind = jnp.where(present, kind, col_count)
    place = jnp.stack([kind, order], axis=2).reshape(-1)
    return send, place


def gather_top(piece, row_count, row_index, panel_blocks):
    if row_count == panel_blocks:
        return lax.all_gather(piece, "row", axis=0, tiled=True)
    ids = jnp.arange(panel_blocks, dtype=jnp.int32)
    kept = jnp.where((ids == row_index)[:, None, None], piece[None], 0.0)
    return lax.psum(kept, "row").reshape(panel_blocks * piece.shape[0], piece.shape[1])


def body(front, updates, maps):
    row_count = lax.axis_size("row")
    col_count = lax.axis_size("col")
    row_index = lax.axis_index("row")
    col_index = lax.axis_index("col")
    front = front.reshape(front.shape[0], 1, *front.shape[2:4], front.shape[5])
    blk, part_cols = front.shape[2], front.shape[3]
    child_cols = updates.shape[4]
    cap = child_cols // 2
    panel_blocks = NP * col_count
    send, place = tables(maps, col_index, col_count, child_cols, part_cols, cap)
    outgoing = pack(send, updates, cap)
    received = []
    for turn in range(1, col_count):
        pairs = [(c, (c + turn) % col_count) for c in range(col_count)]
        received.append(lax.ppermute(outgoing[turn - 1], "col", pairs))
    matrix = assemble(place, front, updates, received)
    panel = jnp.concatenate(
        [
            lax.all_gather(matrix[:, s * blk : (s + 1) * blk], "col", axis=1, tiled=True)
            for s in range(NP)
        ],
        axis=1,
    )
    top = gather_top(matrix[:blk], row_count, row_index, panel_blocks)
    square = gather_top(panel[:blk], row_count, row_index, panel_blocks)
    lower, inverse = factorize(square, blk)
    high, low = right_side(inverse, top, NP * blk, 2 * blk)
    where = jnp.stack([row_index, col_index]).astype(jnp.int32)
    result = finish(where, panel, matrix, inverse, lower, high, low, row_count, col_count, blk)
    return result.reshape(front.shape[0], 1, blk, part_cols, 1, blk)


def solution(mesh):
    return jax.shard_map(
        body,
        mesh=mesh,
        in_specs=(
            P(None, "row", None, None, "col", None),
            P(None, None, "row", None, None, "col", None),
            P(),
        ),
        out_specs=P(None, "row", None, None, "col", None),
        check_vma=False,
    )
```

```python
import functools

import jax
import jax.numpy as jnp
from jax import lax
from jax.experimental import pallas as pl
from jax.experimental.pallas import tpu as pltpu
from jax.sharding import PartitionSpec as P

NP = 2
highest = lax.Precision.HIGHEST
VMEM_LIMIT = 56 * 1024 * 1024


def split(value):
    high = value.astype(jnp.bfloat16)
    low = (value - high.astype(jnp.float32)).astype(jnp.bfloat16)
    return high, low


def dims(transposed):
    return (((1,), (1 if transposed else 0,)), ((), ()))


def product3(left_pair, right_pair, transposed=False):
    def one(a, b):
        return lax.dot_general(a, b, dims(transposed), preferred_element_type=jnp.float32)

    return (
        one(left_pair[0], right_pair[0])
        + one(left_pair[0], right_pair[1])
        + one(left_pair[1], right_pair[0])
    )


def product(a, b, transposed=False):
    return lax.dot_general(
        a, b, dims(transposed), precision=highest, preferred_element_type=jnp.float32
    )


def pack_kernel(child_cols, cap, blk, table, updates_ref, one_ref, two_ref, three_ref):
    for turn, out_ref in enumerate((one_ref, two_ref, three_ref)):
        for member in range(2):
            for slot in range(cap):
                source = table[(turn + 1) * 2 * cap + member * cap + slot]
                out_ref[member * cap + slot] = updates_ref[
                    member, 0, pl.ds(source, blk, stride=child_cols), :
                ]


def pack(table, updates, cap, begin, count):
    part_rows, blk, child_cols = updates.shape[1], updates.shape[3], updates.shape[4]
    flat = updates.reshape(2, part_rows, blk * child_cols, blk)
    return pl.pallas_call(
        functools.partial(pack_kernel, child_cols, cap, blk),
        grid_spec=pltpu.PrefetchScalarGridSpec(
            num_scalar_prefetch=1,
            grid=(count,),
            in_specs=[
                pl.BlockSpec((2, 1, blk * child_cols, blk), lambda a, t: (0, a + begin, 0, 0))
            ],
            out_specs=[pl.BlockSpec((2 * cap, blk, blk), lambda a, t: (0, a, 0))] * 3,
        ),
        out_shape=[jax.ShapeDtypeStruct((2 * cap, count * blk, blk), jnp.float32)] * 3,
        compiler_params=pltpu.CompilerParams(vmem_limit_bytes=VMEM_LIMIT),
        name="pack",
    )(table, flat)


def add_children(out_ref, table, front_ref, updates_ref, received, slots, part_cols, child_cols, blk):
    for slot in slots:
        cols = slice(slot * blk, (slot + 1) * blk)
        out_ref[:, cols] = front_ref[0, pl.ds(slot, blk, stride=part_cols), :]
        for member in range(2):
            turn = table[(member * part_cols + slot) * 2]
            index = table[(member * part_cols + slot) * 2 + 1]

            @pl.when(turn == 0)
            def _():
                out_ref[:, cols] += updates_ref[member, 0, pl.ds(index, blk, stride=child_cols), :]

            for step in range(3):

                @pl.when(turn == step + 1)
                def _():
                    out_ref[:, cols] += received[step][index]


def assemble(table, front, updates, received, begin, count, width):
    part_rows, blk, part_cols = front.shape[0], front.shape[2], front.shape[3]
    child_cols = updates.shape[4]
    slots = received[0].shape[0]

    def kernel(table, front_ref, updates_ref, one, two, three, out_ref):
        add_children(
            out_ref, table, front_ref, updates_ref, (one, two, three),
            range(width), part_cols, child_cols, blk,
        )

    return pl.pallas_call(
        kernel,
        grid_spec=pltpu.PrefetchScalarGridSpec(
            num_scalar_prefetch=1,
            grid=(count,),
            in_specs=[
                pl.BlockSpec((1, blk * part_cols, blk), lambda a, t: (a + begin, 0, 0)),
                pl.BlockSpec((2, 1, blk * child_cols, blk), lambda a, t: (0, a + begin, 0, 0)),
            ]
            + [pl.BlockSpec((slots, blk, blk), lambda a, t: (0, a, 0))] * 3,
            out_specs=pl.BlockSpec((blk, width * blk), lambda a, t: (a, 0)),
        ),
        out_shape=jax.ShapeDtypeStruct((count * blk, width * blk), jnp.float32),
        compiler_params=pltpu.CompilerParams(vmem_limit_bytes=VMEM_LIMIT),
        name="assemble",
    )(
        table,
        front.reshape(part_rows, blk * part_cols, blk),
        updates.reshape(2, part_rows, blk * child_cols, blk),
        *received,
    )


def eliminate(block):
    size = block.shape[0]
    row_ids = lax.broadcasted_iota(jnp.int32, (size, size), 0)
    col_ids = lax.broadcasted_iota(jnp.int32, (size, size), 1)
    tiles = size // 8
    upper = [block[8 * t : 8 * t + 8, :] for t in range(tiles)]
    start = (row_ids == col_ids).astype(jnp.float32)
    solved = [start[8 * t : 8 * t + 8, :] for t in range(tiles)]
    local = lax.broadcasted_iota(jnp.int32, (8, size), 0)
    for j in range(size):
        home, inner = j // 8, j % 8
        pivot_row = upper[home][inner : inner + 1, :]
        solved_row = solved[home][inner : inner + 1, :]
        scale = 1.0 / pivot_row[:, j : j + 1]
        for t in range(home, tiles):
            if t == home and inner == 7:
                continue
            factor = upper[t][:, j : j + 1] * scale
            if t == home:
                factor = jnp.where(local[:, :1] > inner, factor, 0.0)
            upper[t] = upper[t] - factor * pivot_row
            solved[t] = solved[t] - factor * solved_row
    upper = jnp.concatenate(upper, axis=0)
    solved = jnp.concatenate(solved, axis=0)
    diagonal = jnp.sum(jnp.where(row_ids == col_ids, upper, 0.0), axis=1, keepdims=True)
    scale = 1.0 / jnp.sqrt(diagonal)
    lower = jnp.where(col_ids >= row_ids, upper * scale, 0.0).T
    return lower, solved * scale


def factor_kernel(blk, square_ref, lower_ref, inverse_ref, work):
    size = square_ref.shape[0]
    count = size // blk
    work[...] = square_ref[...]
    lower_ref[...] = jnp.zeros_like(lower_ref)
    inverse_ref[...] = jnp.zeros_like(inverse_ref)
    rows = lax.broadcasted_iota(jnp.int32, (size, blk), 0)

    def step(k, carry):
        begin = pl.multiple_of(k * blk, blk)
        here = pl.ds(begin, blk)
        diag_lower, diag_inverse = eliminate(work[here, here])
        inverse_ref[here, here] = diag_inverse
        column = product(work[:, here], diag_inverse, True)
        column = jnp.where(rows >= begin + blk, column, 0.0)
        lower_ref[:, here] = column
        lower_ref[here, here] = diag_lower
        for q in range(0, size, 256):
            piece = slice(q, q + 256)

            @pl.when(q + 256 > begin + blk)
            def _():
                work[piece, :] -= product(lower_ref[piece, here] * (rows[piece] >= begin + blk), column, True)

        return carry

    lax.fori_loop(0, count, step, 0)

    def substitute(i, carry):
        begin = pl.multiple_of(i * blk, blk)
        here = pl.ds(begin, blk)
        cols = lax.broadcasted_iota(jnp.int32, (blk, size), 1)
        diag_inverse = inverse_ref[here, here]
        strip = jnp.where(cols < begin, lower_ref[here, :], 0.0)
        total = product(strip, inverse_ref[...])
        update = product(diag_inverse, total)
        inverse_ref[here, :] -= update
        return carry

    lax.fori_loop(1, count, substitute, 0)


def factorize(square, blk):
    size = square.shape[0]
    shape = jax.ShapeDtypeStruct((size, size), jnp.float32)
    return pl.pallas_call(
        functools.partial(factor_kernel, blk),
        out_shape=[shape, shape],
        scratch_shapes=[pltpu.VMEM((size, size), jnp.float32)],
        compiler_params=pltpu.CompilerParams(vmem_limit_bytes=VMEM_LIMIT),
        cost_estimate=pl.CostEstimate(flops=size, bytes_accessed=size, transcendentals=0),
        name="factorize",
    )(square)


def right_kernel(inverse_ref, top_ref, high_ref, low_ref, inv_high, inv_low):
    @pl.when(pl.program_id(0) == 0)
    def _():
        inv_high[...], inv_low[...] = split(inverse_ref[...])

    result = product3((inv_high[...], inv_low[...]), split(top_ref[...]))
    high_ref[...], low_ref[...] = split(result)


def right_side(inverse, top, tile):
    size, cols = top.shape
    out = jax.ShapeDtypeStruct((size, cols), jnp.bfloat16)
    return pl.pallas_call(
        right_kernel,
        grid=(cols // tile,),
        in_specs=[
            pl.BlockSpec((size, size), lambda n: (0, 0)),
            pl.BlockSpec((size, tile), lambda n: (0, n)),
        ],
        out_specs=[pl.BlockSpec((size, tile), lambda n: (0, n))] * 2,
        out_shape=[out, out],
        scratch_shapes=[pltpu.VMEM((size, size), jnp.bfloat16)] * 2,
        compiler_params=pltpu.CompilerParams(vmem_limit_bytes=VMEM_LIMIT),
        name="right",
    )(inverse, top)


def finish_kernel(
    part_cols, child_cols, blk, row_count, col_count, first, table, place,
    panel_ref, front_ref, updates_ref, one, two, three, inverse_ref, lower_ref, high_ref, low_ref,
    out_ref, inv_high, inv_low, left_ref, sum_ref,
):
    step = pl.program_id(0)
    block_row = step * row_count + place[0]
    panel_blocks = NP * col_count
    inside = block_row < panel_blocks
    columns = [pl.multiple_of((s * col_count + place[1]) * blk, blk) for s in range(NP)]

    @pl.when(step == 0)
    def _():
        inv_high[...], inv_low[...] = split(inverse_ref[...])

    @pl.when(jnp.logical_not(inside))
    def _():
        add_children(
            sum_ref, table, front_ref, updates_ref, (one, two, three),
            range(NP, part_cols), part_cols, child_cols, blk,
        )
        panel = jnp.concatenate(
            [
                panel_ref[c, :, s * blk : (s + 1) * blk]
                for s in range(NP)
                for c in range(col_count)
            ],
            axis=1,
        )
        left_ref[...] = product3(split(panel), (inv_high[...], inv_low[...]), True)
        left_pair = split(left_ref[...])
        for pair in range(NP, part_cols, 2):
            cols = slice((pair - NP) * blk, (pair - NP + 2) * blk)
            trailing = product3(left_pair, (high_ref[:, cols], low_ref[:, cols]))
            updated = sum_ref[:, pair * blk : (pair + 2) * blk] - trailing
            for half in range(2):
                out_ref[0, pl.ds(pair + half, blk, stride=part_cols), :] = updated[
                    :, half * blk : (half + 1) * blk
                ]
        for s in range(NP):
            out_ref[0, pl.ds(s, blk, stride=part_cols), :] = left_ref[:, pl.ds(columns[s], blk)]

    @pl.when(inside)
    def _():
        out_ref[...] = jnp.zeros_like(out_ref)
        begin = pl.multiple_of(block_row * blk, blk)
        for s in range(NP):
            out_ref[0, pl.ds(s, blk, stride=part_cols), :] = lower_ref[
                pl.ds(begin, blk), pl.ds(columns[s], blk)
            ]


def finish(table, place, panel, front, updates, received, inverse, lower, high, low, row_count, first):
    part_rows, blk, part_cols = front.shape[0], front.shape[2], front.shape[3]
    child_cols = updates.shape[4]
    size = inverse.shape[0]
    slots = received[0].shape[0]
    col_count = panel.shape[0]

    def resident(shape):
        return pl.BlockSpec(shape, lambda a, t, p: (0, 0), pipeline_mode=pl.Buffered(1))

    def late(a, t, p):
        return (0, jnp.maximum(a - first, 0), 0)

    return pl.pallas_call(
        functools.partial(finish_kernel, part_cols, child_cols, blk, row_count, col_count, first),
        grid_spec=pltpu.PrefetchScalarGridSpec(
            num_scalar_prefetch=2,
            grid=(part_rows,),
            in_specs=[
                pl.BlockSpec((col_count, blk, NP * blk), late),
                pl.BlockSpec((1, blk * part_cols, blk), lambda a, t, p: (a, 0, 0)),
                pl.BlockSpec((2, 1, blk * child_cols, blk), lambda a, t, p: (0, a, 0, 0)),
            ]
            + [pl.BlockSpec((slots, blk, blk), late)] * 3
            + [
                resident((size, size)),
                resident((size, size)),
                resident(high.shape),
                resident(low.shape),
            ],
            out_specs=pl.BlockSpec((1, blk * part_cols, blk), lambda a, t, p: (a, 0, 0)),
            scratch_shapes=[
                pltpu.VMEM((size, size), jnp.bfloat16),
                pltpu.VMEM((size, size), jnp.bfloat16),
                pltpu.VMEM((blk, size), jnp.float32),
                pltpu.VMEM((blk, part_cols * blk), jnp.float32),
            ],
        ),
        out_shape=jax.ShapeDtypeStruct((part_rows, blk * part_cols, blk), jnp.float32),
        compiler_params=pltpu.CompilerParams(vmem_limit_bytes=VMEM_LIMIT),
        name="finish",
    )(
        table, place, panel,
        front.reshape(part_rows, blk * part_cols, blk),
        updates.reshape(2, part_rows, blk * child_cols, blk),
        *received, inverse, lower, high, low,
    )


def tables(maps, col_index, col_count, child_cols, part_cols, cap):
    offsets = maps[:, ::col_count] - col_count * jnp.arange(child_cols, dtype=jnp.int32)[None, :]
    turn = offsets % col_count
    groups = jnp.arange(child_cols, dtype=jnp.int32)
    same = (turn[:, :, None] == turn[:, None, :]) & (groups[None, None, :] < groups[None, :, None])
    rank = jnp.sum(same.astype(jnp.int32), axis=2)
    turns = jnp.arange(col_count, dtype=jnp.int32)
    slots = jnp.arange(cap, dtype=jnp.int32)
    hot = (turn[None, :, None, :] == turns[:, None, None, None]) & (
        rank[None, :, None, :] == slots[None, None, :, None]
    )
    send = jnp.sum(jnp.where(hot, groups[None, None, None, :], 0), axis=3).reshape(-1)
    parents = jnp.arange(part_cols, dtype=jnp.int32) * col_count + col_index
    match = maps[:, None, :] == parents[None, :, None]
    spread = jnp.repeat(groups, col_count)
    group = jnp.sum(jnp.where(match, spread[None, None, :], 0), axis=2)
    present = jnp.any(match, axis=2)
    pick = group[:, :, None] == groups[None, None, :]
    kind = jnp.sum(jnp.where(pick, turn[:, None, :], 0), axis=2)
    order = jnp.sum(jnp.where(pick, rank[:, None, :], 0), axis=2)
    order = jnp.where(kind == 0, group, order + cap * jnp.arange(2, dtype=jnp.int32)[:, None])
    kind = jnp.where(present, kind, col_count)
    place = jnp.stack([kind, order], axis=2).reshape(-1)
    return send, place


def gather_top(piece, row_count, row_index, panel_blocks):
    if row_count == panel_blocks:
        return lax.all_gather(piece, "row", axis=0, tiled=True)
    ids = jnp.arange(panel_blocks, dtype=jnp.int32)
    kept = jnp.where((ids == row_index)[:, None, None], piece[None], 0.0)
    return lax.psum(kept, "row").reshape(panel_blocks * piece.shape[0], piece.shape[1])


def body(front, updates, maps):
    row_count = lax.axis_size("row")
    col_count = lax.axis_size("col")
    row_index = lax.axis_index("row")
    col_index = lax.axis_index("col")
    front = front.reshape(front.shape[0], 1, *front.shape[2:4], front.shape[5])
    blk, part_cols = front.shape[2], front.shape[3]
    child_cols = updates.shape[4]
    cap = child_cols // 2
    panel_blocks = NP * col_count
    send, place = tables(maps, col_index, col_count, child_cols, part_cols, cap)
    part_rows = front.shape[0]
    first = 1 if part_rows > 1 and row_count == panel_blocks else part_rows

    def exchange(outgoing):
        return [
            lax.ppermute(
                outgoing[turn - 1], "col", [(c, (c + turn) % col_count) for c in range(col_count)]
            )
            for turn in range(1, col_count)
        ]

    early = exchange(pack(send, updates, cap, 0, first))
    if first < part_rows:
        outgoing = pack(send, updates, cap, first, part_rows - first)
        early, outgoing = lax.optimization_barrier((early, outgoing))
        received = exchange(outgoing)
    else:
        received = early
    head = assemble(place, front, updates, early, 0, 1, part_cols)
    square = jnp.concatenate(
        [
            lax.all_gather(head[:, s * blk : (s + 1) * blk], "col", axis=1, tiled=True)
            for s in range(NP)
        ],
        axis=1,
    )
    square = gather_top(square, row_count, row_index, panel_blocks)
    rest, square = lax.optimization_barrier((head[:, NP * blk :], square))
    top = gather_top(rest, row_count, row_index, panel_blocks)
    lower, inverse = factorize(square, blk)
    high, low = right_side(inverse, top, 2 * blk)
    received, high, low = lax.optimization_barrier((received, high, low))
    late = first if first < part_rows else 0
    panel = assemble(place, front, updates, received, late, part_rows - late, NP)
    panel = lax.all_gather(panel, "col", axis=0)
    where = jnp.stack([row_index, col_index]).astype(jnp.int32)
    result = finish(
        place, where, panel, front, updates, received, inverse, lower, high, low, row_count, late
    )
    return result.reshape(front.shape[0], 1, blk, part_cols, 1, blk)


def solution(mesh):
    return jax.shard_map(
        body,
        mesh=mesh,
        in_specs=(
            P(None, "row", None, None, "col", None),
            P(None, None, "row", None, None, "col", None),
            P(),
        ),
        out_specs=P(None, "row", None, None, "col", None),
        check_vma=False,
    )
```
